32 devices in a mesh: dp: 16 (over z, y, core), tensor: 2 (over x).
Axes of the slice: x: 2, y: 2, z: 4, core: 2. Of those that a mesh axis runs over, the one named last changes fastest.
Arguments:
- tokens: bfloat16 [16384, 1024], P(('dp', 'tensor')), may hold values from -6 to 6
- doc_ids: int32 [16384], P('dp'), may hold values from 0 to 4, as said below
- w_qkv: bfloat16 [3, 1024, 1024], P(None, None, 'tensor'), may hold values from -0.1875 to 0.1875
- qv_bias: float32 [2, 1024], P(None, 'tensor'), may hold values from -3 to 3
- out_weight: bfloat16 [1024, 1024], P('tensor'), may hold values from -3 to 3
- out_biases: float32 [2, 1024], replicated, may hold values from -3 to 3
- ln_gains: float32 [2, 1024], replicated, may hold values from 0.1 to 1.9
- ln_shifts: float32 [2, 1024], replicated, may hold values from -3 to 3
- up_weight: bfloat16 [1024, 4096], P(None, 'tensor'), may hold values from -0.1875 to 0.1875
- up_bias: float32 [4096], P('tensor'), may hold values from -3 to 3
- down_weight: bfloat16 [4096, 1024], P('tensor'), may hold values from -0.09375 to 0.09375
- cotangent: bfloat16 [16384, 1024], P(('dp', 'tensor')), may hold values from -6 to 6
Outputs:
- out: bfloat16 [16384, 1024], P(('dp', 'tensor'))
- grad_input: bfloat16 [16384, 1024], P(('dp', 'tensor'))
- grad_qkv: float32 [3, 1024, 1024], P(None, None, 'tensor')
- grad_qv_bias: float32 [2, 1024], P(None, 'tensor')
- grad_out_weight: float32 [1024, 1024], P('tensor')
- grad_out_biases: float32 [2, 1024], replicated
- grad_ln_gains: float32 [2, 1024], replicated
- grad_ln_shifts: float32 [2, 1024], replicated
- grad_up_weight: float32 [1024, 4096], P(None, 'tensor')
- grad_up_bias: float32 [4096], P('tensor')
- grad_down_weight: float32 [4096, 1024], P('tensor')
The draws below stay inside these ranges and needn't reach their ends.
Inputs may be any that keep to these rules, and one draw needn't show every extreme that they name: `doc_ids`: within each buffer (rows 1024 * b to 1024 * (b + 1) - 1) the numbers never fall; the value 4 marks padding, which stands only at a buffer's end; at least 512 slots of every buffer are not padding; a sequence is a run of one number below 4 in one buffer, of 1 to 1024 slots, and some buffer holds a single sequence of 1024 slots.
All inputs are finite; a program needn't handle non-finite values.
Results may differ from the reference program's by a relative error of at most 0.03.
Values may be sent and summed in bfloat16 or wider, within the bound.
No kernel may reach another device: no remote copies, remote signals or barrier semaphores. Data moves between devices by JAX's collectives and lax.ppermute only.
A program may use at most 256 MiB of HBM per device.

```python
import math
import jax
import jax.numpy as jnp
from jax import lax

D = 1024
H = 16
FF = 4096
TOK_DEV = 1024
DOCS_DEV = 4
TOKENS = 16384
N_DP = 16
N_TENSOR = 2


def draw_doc_ids(key, part):
    buffers = TOKENS // TOK_DEV
    key_fill, key_cuts, key_order = jax.random.split(key, 3)
    fill = jax.random.randint(key_fill, (buffers,), TOK_DEV // 2, TOK_DEV + 1)
    cuts = jax.random.randint(key_cuts, (buffers, DOCS_DEV - 1), 1, TOK_DEV)
    order = jax.random.permutation(key_order, buffers)
    slots = jnp.arange(TOK_DEV, dtype=jnp.int32)
    numbers = jnp.sum((cuts[:, None, :] <= slots[None, :, None]).astype(jnp.int32), axis=2)
    buffer_pos = jnp.arange(buffers, dtype=jnp.int32)
    single = buffer_pos == order[0]
    halved = buffer_pos == order[1]
    numbers = jnp.where(single[:, None], 0, numbers)
    fill = jnp.where(single, TOK_DEV, jnp.where(halved, TOK_DEV // 2, fill))
    numbers = jnp.where(slots[None, :] < fill[:, None], numbers, DOCS_DEV)
    return numbers.reshape(TOKENS).astype(jnp.int32)


def level_of(rng, shape, shards, low, top_value):
    def one(dim, shards_of):
        heights = jax.random.uniform(jax.random.fold_in(jax.random.fold_in(rng, 6), dim), (shards_of,), jnp.float32, low / len(shards), top_value / len(shards))
        return jnp.repeat(jnp.exp(heights), shape[dim] // shards_of).reshape((-1,) + (1,) * (len(shape) - dim - 1))

    loudness = one(*shards[0])
    for cut in shards[1:]:
        loudness = loudness * one(*cut)
    return loudness


def scatter_about(stream_key, extent, scale, limit, shards=(), kind=jnp.bfloat16):
    entries = scale * jax.random.normal(stream_key, extent, jnp.float32)
    if shards:
        entries = entries * level_of(stream_key, extent, shards, -0.22, 0.18)
    return jnp.clip(entries, -limit, limit).astype(kind)


def setup_inputs(seed: int = 0) -> dict:
    seeds = jax.random.split(jax.random.key(seed), 13)
    tokens = scatter_about(seeds[0], (TOKENS, D), 1.0, 6.0, ((0, 32),))
    doc_ids = draw_doc_ids(jax.random.fold_in(seeds[12], 71), 0)
    w_qkv = scatter_about(seeds[2], (3, D, D), D ** -0.5, 0.1875, ((2, 2),))
    qv_bias = scatter_about(seeds[3], (2, D), 0.5, 3.0, ((1, 2),), jnp.float32)
    out_weight = scatter_about(seeds[4], (D, D), (max(1, 4 * D // TOK_DEV)) ** -0.5, 3.0, ((0, 2),))
    out_biases = scatter_about(seeds[5], (2, D), 0.5, 3.0, (), jnp.float32)
    ln_gains = jnp.clip(1.0 + 0.18 * jax.random.normal(seeds[6], (2, D), jnp.float32), 0.1, 1.9)
    ln_shifts = scatter_about(seeds[7], (2, D), 0.5, 3.0, (), jnp.float32)
    up_weight = scatter_about(seeds[8], (D, FF), D ** -0.5, 0.1875, ((1, 2),))
    up_bias = scatter_about(seeds[9], (FF,), 0.5, 3.0, ((0, 2),), jnp.float32)
    down_weight = scatter_about(seeds[10], (FF, D), FF ** -0.5, 0.09375, ((0, 2),))
    cotangent = scatter_about(seeds[11], (TOKENS, D), 1.0, 6.0, ((0, 32),))
    return dict(tokens=tokens, doc_ids=doc_ids, w_qkv=w_qkv, qv_bias=qv_bias, out_weight=out_weight, out_biases=out_biases, ln_gains=ln_gains, ln_shifts=ln_shifts, up_weight=up_weight, up_bias=up_bias, down_weight=down_weight, cotangent=cotangent)


@jax.custom_vjp
def low(v):
    return lax.optimization_barrier(v.astype(jnp.bfloat16)).astype(jnp.float32)

@jax.custom_vjp
def low_back(v):
    return v

def low_keep(v):
    return (low(v), None)

def low_pass(kept, grad):
    return (grad,)

def back_keep(v):
    return (v, None)

def back_low(kept, grad):
    return (low(grad),)
low.defvjp(low_keep, low_pass)
low_back.defvjp(back_keep, back_low)
EPSILON = 1e-06
PRECISE = lax.Precision.HIGHEST

def layer_norm(summed, gain, shift):
    centred = summed - lax.optimization_barrier(jnp.mean(summed, axis=-1, keepdims=True))
    variance = lax.optimization_barrier(jnp.mean(centred * centred, axis=-1, keepdims=True))
    return centred * lax.rsqrt(variance + EPSILON) * gain + shift

def grouped_sum(left, right):
    row_total = left.shape[0]
    group_width = left.shape[1] // N_TENSOR
    left_groups = left.reshape(row_total, N_TENSOR, group_width)
    right_groups = right.reshape(N_TENSOR, group_width, right.shape[1])
    partials = jnp.einsum('sgj,gjd->gsd', left_groups, right_groups, precision=PRECISE)
    return lax.optimization_barrier(jnp.sum(low(partials), axis=0))

def buffer_layer(inputs, doc_rows, params):
    w_qkv, qv_bias, out_weight, out_biases, ln_gains, ln_shifts, up_weight, up_bias, down_weight = params
    row_total = inputs.shape[0]
    head_size = D // H
    projected = jnp.einsum('sd,idc->isc', inputs, w_qkv, precision=PRECISE)
    queries = low(low_back(projected[0] + qv_bias[0])).reshape(row_total, H, head_size)
    keys_all = low(low_back(projected[1])).reshape(row_total, H, head_size)
    values_all = low(low_back(projected[2] + qv_bias[1])).reshape(row_total, H, head_size)
    allowed = doc_rows[:, None] == doc_rows[None, :]
    scores = jnp.einsum('qhc,khc->hqk', queries, keys_all, precision=PRECISE) * (1.0 / math.sqrt(head_size))
    scores = low_back(jnp.where(allowed[None], scores, -1000000000.0))
    weights = low(jax.nn.softmax(scores, axis=-1))
    mixed_heads = jnp.einsum('hqk,khc->qhc', weights, values_all, precision=PRECISE).reshape(row_total, D)
    mixed_heads = low(low_back(mixed_heads))
    attention = low_back(grouped_sum(mixed_heads, out_weight))
    normed = layer_norm(inputs + attention + out_biases[0], ln_gains[0], ln_shifts[0])
    hidden = low_back(jnp.dot(low(normed), up_weight, precision=PRECISE) + up_bias)
    active = low(jax.nn.gelu(hidden, approximate=False))
    branch = low_back(grouped_sum(active, down_weight))
    return layer_norm(normed + branch + out_biases[1], ln_gains[1], ln_shifts[1])

def reference(tokens, doc_ids, w_qkv, qv_bias, out_weight, out_biases, ln_gains, ln_shifts, up_weight, up_bias, down_weight, cotangent):
    params = tuple((item.astype(jnp.float32) for item in (w_qkv, qv_bias, out_weight, out_biases, ln_gains, ln_shifts, up_weight, up_bias, down_weight)))
    inputs = tokens.astype(jnp.float32).reshape(N_DP, TOK_DEV, D)
    doc_table = doc_ids.reshape(N_DP, TOK_DEV)
    valid = (doc_table < DOCS_DEV).astype(jnp.float32)
    seed_grad = cotangent.astype(jnp.float32).reshape(N_DP, TOK_DEV, D) * valid[:, :, None]
    checked = jax.checkpoint(buffer_layer)

    def forward(inputs_all, params_all):

        def visit(state, item):
            return (state, checked(item[0], item[1], params_all))
        return lax.scan(visit, jnp.zeros((), jnp.float32), (inputs_all, doc_table))[1]
    result, pullback = jax.vjp(forward, inputs, params)
    grad_inputs, grads = pullback(seed_grad)
    return (result.reshape(TOKENS, D).astype(jnp.bfloat16), grad_inputs.reshape(TOKENS, D).astype(jnp.bfloat16), grads[0], grads[1], grads[2], grads[3], grads[4], grads[5], grads[6], grads[7], grads[8])
```

```python
import functools
import math

import jax
import jax.numpy as jnp
from jax import lax
from jax.experimental import pallas as pl
from jax.experimental.pallas import tpu as pltpu
from jax.sharding import PartitionSpec as P

D = 1024
H = 16
DOCS_DEV = 4


EPSILON = 1e-06
ROOT_HALF = 0.7071067811865476
GAUSS_NORM = 0.3989422804014327
NT = (((1,), (1,)), ((), ()))
VMEM_ASK = 48 << 20


def norm_forward(summed, gain, shift):
    centred = summed - jnp.mean(summed, axis=-1, keepdims=True)
    inverse = lax.rsqrt(jnp.mean(centred * centred, axis=-1, keepdims=True) + EPSILON)
    unit = centred * inverse
    return (unit * gain + shift, unit, inverse)


def norm_backward(upstream, unit, inverse, gain):
    spread = upstream * gain
    inner = (
        spread
        - jnp.mean(spread, axis=-1, keepdims=True)
        - unit * jnp.mean(spread * unit, axis=-1, keepdims=True)
    )
    return (inner * inverse, jnp.sum(upstream * unit, axis=0), jnp.sum(upstream, axis=0))


def attn_forward_kernel(block, scale, own_ref, rest_ref, seen_ref, bar_ref, *refs):
    mixed_ref, lse_ref = refs[-2:]
    lane = lax.broadcasted_iota(jnp.int32, (1, 128), 1)
    rows = own_ref.shape[1] + rest_ref.shape[1]
    keys = jnp.concatenate([own_ref[1], rest_ref[1]], axis=0)
    values_t = jnp.concatenate([own_ref[2], rest_ref[2]], axis=0).T
    queries = jnp.concatenate([own_ref[0], rest_ref[0]], axis=0) * jnp.bfloat16(scale)
    half = [(lane // 64) == h for h in range(2)]
    keys_of = [jnp.where(half[h], keys, bar_ref[...]) for h in range(2)]
    for first in range(0, rows, block):
        span = slice(first, first + block)
        out_t = []
        for h in range(2):
            query = jnp.where(half[h], queries[span], seen_ref[span])
            scores = lax.dot_general(keys_of[h], query, NT, preferred_element_type=jnp.float32)
            top = jnp.max(scores, axis=0, keepdims=True)
            expd = jnp.exp(scores - top)
            total = jnp.sum(expd, axis=0, keepdims=True)
            mixed = jnp.dot(
                values_t[64 * h : 64 * h + 64],
                expd.astype(jnp.bfloat16),
                preferred_element_type=jnp.float32,
            )
            out_t.append(mixed / total)
            lse_ref[0, h : h + 1, span] = top + jnp.log(total)
        mixed_ref[span] = jnp.concatenate(out_t, axis=0).T.astype(jnp.bfloat16)


def attn_backward_kernel(
    block,
    scale,
    own_ref,
    rest_ref,
    up_own_ref,
    up_rest_ref,
    mixed_ref,
    lse_ref,
    seen_ref,
    bar_ref,
    *refs,
):
    grad_own_ref, grad_rest_ref, key_acc, value_acc = refs[-4:]
    lane = lax.broadcasted_iota(jnp.int32, (1, 128), 1)
    rows_own = own_ref.shape[1]
    rows = rows_own + rest_ref.shape[1]
    keys = jnp.concatenate([own_ref[1], rest_ref[1]], axis=0)
    values = jnp.concatenate([own_ref[2], rest_ref[2]], axis=0)
    keys_t = keys.T
    half = [(lane // 64) == h for h in range(2)]
    keys_of = [jnp.where(half[h], keys, bar_ref[...]) for h in range(2)]
    nothing = jnp.zeros((block, 128), jnp.bfloat16)
    for first in range(0, rows, block):
        span = slice(first, first + block)
        if first < rows_own:
            here, source, up_ref, out_ref = span, own_ref, up_own_ref, grad_own_ref
        else:
            here = slice(first - rows_own, first - rows_own + block)
            source, up_ref, out_ref = rest_ref, up_rest_ref, grad_rest_ref
        query_rows = source[0, here]
        up_rows = up_ref[here]
        product = (up_rows.astype(jnp.float32) * mixed_ref[span].astype(jnp.float32)).T
        query_grad_t = []
        for h in range(2):
            query = jnp.where(half[h], query_rows * jnp.bfloat16(scale), seen_ref[span])
            up = jnp.where(half[h], up_rows, nothing)
            scores = lax.dot_general(keys_of[h], query, NT, preferred_element_type=jnp.float32)
            probs = jnp.exp(scores - lse_ref[0, h : h + 1, span])
            spread = lax.dot_general(values, up, NT, preferred_element_type=jnp.float32)
            inner = jnp.sum(product[64 * h : 64 * h + 64], axis=0, keepdims=True)
            score_grad = (probs * (spread - inner)).astype(jnp.bfloat16)
            value_part = jnp.dot(probs.astype(jnp.bfloat16), up, preferred_element_type=jnp.float32)
            key_part = jnp.dot(
                score_grad, jnp.where(half[h], query_rows, nothing), preferred_element_type=jnp.float32
            )
            if first == 0 and h == 0:
                value_acc[...] = value_part
                key_acc[...] = key_part
            else:
                value_acc[...] += value_part
                key_acc[...] += key_part
            query_grad_t.append(
                jnp.dot(keys_t[64 * h : 64 * h + 64], score_grad, preferred_element_type=jnp.float32)
            )
        out_ref[0, here] = (jnp.concatenate(query_grad_t, axis=0).T * scale).astype(jnp.bfloat16)
    key_low = (key_acc[...] * scale).astype(jnp.bfloat16)
    value_low = value_acc[...].astype(jnp.bfloat16)
    grad_own_ref[1] = key_low[:rows_own]
    grad_rest_ref[1] = key_low[rows_own:]
    grad_own_ref[2] = value_low[:rows_own]
    grad_rest_ref[2] = value_low[rows_own:]


def attn_forward(own, rest, seen, bar, scale, block, start, count, previous=()):
    rows_own, rows_rest, width = own.shape[1], rest.shape[1], own.shape[2]
    rows = rows_own + rows_rest
    return pl.pallas_call(
        functools.partial(attn_forward_kernel, block, scale),
        grid=(count,),
        in_specs=[
            pl.BlockSpec((3, rows_own, 128), lambda p: (0, 0, p + start)),
            pl.BlockSpec((3, rows_rest, 128), lambda p: (0, 0, p + start)),
            pl.BlockSpec((rows, 128), lambda p: (0, 0)),
            pl.BlockSpec((rows, 128), lambda p: (0, 0)),
        ]
        + [pl.BlockSpec(memory_space=pl.ANY)] * len(previous),
        out_specs=[
            pl.BlockSpec((rows, 128), lambda p: (0, p + start)),
            pl.BlockSpec((1, 8, rows), lambda p: (p + start, 0, 0)),
        ],
        out_shape=[
            jax.ShapeDtypeStruct((rows, width), jnp.bfloat16),
            jax.ShapeDtypeStruct((width // 128, 8, rows), jnp.float32),
        ],
        input_output_aliases={4: 0, 5: 1} if previous else {},
        compiler_params=pltpu.CompilerParams(vmem_limit_bytes=VMEM_ASK),
        cost_estimate=pl.CostEstimate(
            flops=count * 16 * 256 * rows * rows,
            transcendentals=count * 2 * rows * rows,
            bytes_accessed=count * 10 * 128 * rows,
        ),
        name="attn_forward",
    )(own, rest, seen, bar, *previous)


def attn_backward(
    own, rest, up_own, up_rest, mixed, lse, seen, bar, scale, block, start, count, previous=()
):
    rows_own, rows_rest, width = own.shape[1], rest.shape[1], own.shape[2]
    rows = rows_own + rows_rest
    return pl.pallas_call(
        functools.partial(attn_backward_kernel, block, scale),
        grid=(count,),
        in_specs=[
            pl.BlockSpec((3, rows_own, 128), lambda p: (0, 0, p + start)),
            pl.BlockSpec((3, rows_rest, 128), lambda p: (0, 0, p + start)),
            pl.BlockSpec((rows_own, 128), lambda p: (0, p + start)),
            pl.BlockSpec((rows_rest, 128), lambda p: (0, p + start)),
            pl.BlockSpec((rows, 128), lambda p: (0, p + start)),
            pl.BlockSpec((1, 8, rows), lambda p: (p + start, 0, 0)),
            pl.BlockSpec((rows, 128), lambda p: (0, 0)),
            pl.BlockSpec((rows, 128), lambda p: (0, 0)),
        ]
        + [pl.BlockSpec(memory_space=pl.ANY)] * len(previous),
        out_specs=[
            pl.BlockSpec((3, rows_own, 128), lambda p: (0, 0, p + start)),
            pl.BlockSpec((3, rows_rest, 128), lambda p: (0, 0, p + start)),
        ],
        out_shape=[
            jax.ShapeDtypeStruct((3, rows_own, width), jnp.bfloat16),
            jax.ShapeDtypeStruct((3, rows_rest, width), jnp.bfloat16),
        ],
        input_output_aliases={8: 0, 9: 1} if previous else {},
        scratch_shapes=[pltpu.VMEM((rows, 128), jnp.float32)] * 2,
        compiler_params=pltpu.CompilerParams(vmem_limit_bytes=VMEM_ASK),
        cost_estimate=pl.CostEstimate(
            flops=count * 24 * 256 * rows * rows,
            transcendentals=count * 2 * rows * rows,
            bytes_accessed=count * 18 * 128 * rows,
        ),
        name="attn_backward",
    )(own, rest, up_own, up_rest, mixed, lse, seen, bar, *previous)


def doc_features(docs):
    slot = lax.broadcasted_iota(jnp.int32, (1, 128), 1) % 64
    same = docs[:, None] == slot
    seen = same.astype(jnp.bfloat16)
    bar = jnp.where(same | (slot > 4), 0.0, -(2.0**30)).astype(jnp.bfloat16)
    return seen, bar


def xor_step(array, mask):
    size = lax.axis_size("dp")
    return lax.ppermute(array, "dp", [(i, i ^ mask) for i in range(size)])


def from_rank(array, ahead):
    size = lax.axis_size("tensor")
    return lax.ppermute(array, "tensor", [((i + ahead) % size, i) for i in range(size)])


def exchange(parts):
    size = lax.axis_size("tensor")
    got = [None] * size
    for ahead in range(1, size):
        got[size - ahead] = lax.ppermute(
            parts[ahead], "tensor", [(i, (i + ahead) % size) for i in range(size)]
        )
    return got


def meet(*trees):
    return lax.optimization_barrier(trees)


def spread_kernel(count, order_ref, near_ref, far_ref, out_ref):
    step = pl.program_id(0)
    rows = near_ref.shape[0] // count

    def store(ref):
        for index in range(count):
            offset = pl.multiple_of(order_ref[4 + index] * rows, rows)
            out_ref[pl.ds(offset, rows)] = ref[index * rows : (index + 1) * rows].astype(
                out_ref.dtype
            )

    @pl.when(step < 2)
    def _():
        store(near_ref)

    @pl.when(step > 1)
    def _():
        store(far_ref)


def spread(near, far, place, count, kind):
    rows, columns = near.shape[0] // 2, near.shape[1]
    quarter, inner = lax.div(place, jnp.int32(count)), lax.rem(place, jnp.int32(count))
    order = jnp.concatenate(
        [
            jnp.bitwise_xor(quarter, jnp.arange(4, dtype=jnp.int32)),
            jnp.bitwise_xor(inner, jnp.arange(count, dtype=jnp.int32)),
        ]
    )
    return pl.pallas_call(
        functools.partial(spread_kernel, count),
        grid_spec=pltpu.PrefetchScalarGridSpec(
            num_scalar_prefetch=1,
            grid=(4,),
            in_specs=[
                pl.BlockSpec((rows, columns), lambda step, order: (jnp.minimum(step, 1), 0)),
                pl.BlockSpec((rows, columns), lambda step, order: (jnp.maximum(step - 2, 0), 0)),
            ],
            out_specs=pl.BlockSpec((rows, columns), lambda step, order: (order[step], 0)),
        ),
        out_shape=jax.ShapeDtypeStruct((4 * rows, columns), kind),
        compiler_params=pltpu.CompilerParams(vmem_limit_bytes=VMEM_ASK // 2),
        cost_estimate=pl.CostEstimate(
            flops=0, transcendentals=0, bytes_accessed=24 * rows * columns
        ),
        name="spread_rows",
    )(order, near, far)


def bit_of(dp_pos, mask):
    return jnp.where(lax.bitwise_and(dp_pos, mask) != 0, 1, 0).astype(jnp.int32)


def half_of(array, index):
    rows = array.shape[0] // 2
    return lax.dynamic_slice_in_dim(array, index * rows, rows, 0)


def opening(parts, dp_pos, mask):
    bit = bit_of(dp_pos, mask)
    return [half_of(part, 1 - bit) for part in parts], [half_of(part, bit) for part in parts]


def send(arrays, mask):
    return [xor_step(array, mask) for array in arrays]


def add(keep, got):
    return [
        (a.astype(jnp.float32) + b.astype(jnp.float32)).astype(a.dtype)
        for a, b in zip(keep, got, strict=True)
    ]


def fold(keep, got, dp_pos, mask):
    bit = bit_of(dp_pos, mask)
    away = add([half_of(a, 1 - bit) for a in keep], [half_of(b, 1 - bit) for b in got])
    kept = add([half_of(a, bit) for a in keep], [half_of(b, bit) for b in got])
    return away, kept


def fold_ranks(keep, got):
    total = add(keep, got)
    return [total[0]], exchange(total)[1:]


def add_ranks(keep, got):
    total = keep[0].astype(jnp.float32)
    for piece in got:
        total = total + piece.astype(jnp.float32)
    return total.astype(keep[0].dtype)


def scatter_on(array, dp_pos, masks):
    for mask in masks:
        away, keep = opening([array], dp_pos, mask)
        array = add(keep, send(away, mask))[0]
    return array


def gather_rows(mine, dp_pos, masks):
    for mask in reversed(masks[1:]):
        mine = jnp.concatenate([mine, xor_step(mine, mask)], axis=0)
    place = jnp.int32(0)
    for mask in masks:
        place = 2 * place + bit_of(dp_pos, mask)
    return spread(mine, xor_step(mine, masks[0]), place, 2 ** (len(masks) - 2), jnp.float32)


def butterfly(array, axis):
    size = lax.axis_size(axis)
    mask = 1
    while mask < size:
        array = array + lax.ppermute(array, axis, [(i, i ^ mask) for i in range(size)])
        mask *= 2
    return array


def shards(
    tokens,
    doc_ids,
    w_qkv,
    qv_bias,
    out_weight,
    out_biases,
    ln_gains,
    ln_shifts,
    up_weight,
    up_bias,
    down_weight,
    cotangent,
):
    low = jnp.bfloat16
    rows_own = tokens.shape[0]
    ranks = lax.axis_size("tensor")
    tensor_pos = lax.axis_index("tensor")
    dp_pos = lax.axis_index("dp")
    head_size = D // H
    width = w_qkv.shape[2]
    scale = 1.0 / math.sqrt(head_size)

    count_dp = lax.axis_size("dp")
    masks = [2**k for k in range(count_dp.bit_length() - 1)]
    masks_up = [masks[0], masks[2], masks[1]] + masks[3:]
    others = range(1, ranks)

    rest = [from_rank(tokens, ahead) for ahead in others]
    rest = rest[0] if ranks == 2 else jnp.concatenate(rest, axis=0)
    up_biases = [up_bias] + [from_rank(up_bias, ahead) for ahead in others]
    out_own, up_own, down_own, rest = meet(out_weight, up_weight, down_weight, rest)

    place = 4 * bit_of(dp_pos, 1) + 2 * bit_of(dp_pos, 4) + bit_of(dp_pos, 2)

    def slice_from(weight, pieces, index):
        rows = weight.shape[0] // pieces
        mine = lax.dynamic_slice_in_dim(weight, index * rows, rows, 0)
        return [from_rank(mine, ahead) for ahead in others]

    def joined(groups):
        return [jnp.concatenate(items, axis=0) for items in zip(*groups, strict=True)]

    def corner(by_first, by_second):
        rows = by_first[0].shape[0] // 2
        return (
            [xor_step(item[:rows], 2) for item in by_second],
            [xor_step(item[rows:], 4) for item in by_first],
        )

    out_place = 2 * bit_of(dp_pos, 1) + bit_of(dp_pos, 2)
    out_first, up_first, down_first = (
        slice_from(out_own, 4, out_place),
        slice_from(up_own, 8, place),
        slice_from(down_own, 8, place),
    )
    docs = [
        lax.dynamic_slice_in_dim(
            doc_ids, lax.rem(tensor_pos + ahead, ranks) * rows_own, rows_own, 0
        )
        for ahead in range(ranks)
    ]
    seen, bar = doc_features(jnp.concatenate(docs, axis=0))
    bias = jnp.stack([qv_bias[0], jnp.zeros_like(qv_bias[0]), qv_bias[1]])[:, None, :]

    def project(rows):
        wide = jnp.einsum("sd,idc->isc", rows, w_qkv, preferred_element_type=jnp.float32)
        return (wide + bias).astype(low)

    qkv_own, qkv_rest = project(tokens), project(rest)
    pairs = width // 128
    early = max(1, pairs // 2)
    block = min(512, rows_own)
    mixed_lse = attn_forward(qkv_own, qkv_rest, seen, bar, scale, block, 0, early)
    mixed_lse, out_first, up_first = meet(mixed_lse, out_first, up_first)
    out_second = send(out_first, 2)
    up_second, up_third = send(up_first, 2), send(up_first, 4)
    if pairs > early:
        mixed_lse = attn_forward(
            qkv_own, qkv_rest, seen, bar, scale, block, early, pairs - early, tuple(mixed_lse)
        )
    mixed_lse, out_second, down_first = meet(mixed_lse, out_second, down_first)
    out_half = joined([out_first, out_second])
    out_far = send(out_half, 1)
    down_second, down_third = send(down_first, 2), send(down_first, 4)
    mixed, lse = mixed_lse
    mixed_parts = [mixed[k * rows_own : (k + 1) * rows_own] for k in range(ranks)]
    mixed_got = exchange(mixed_parts)
    mixed_got[0] = mixed_parts[0]
    mixed_got, out_far, up_second, up_third = meet(mixed_got, out_far, up_second, up_third)
    up_corner = corner(up_second, up_third)
    outs = [out_own] + [
        spread(near, far, out_place, 1, low) for near, far in zip(out_half, out_far, strict=True)
    ]
    attention = sum(
        jnp.dot(mixed_got[k], outs[k], preferred_element_type=jnp.float32) for k in range(ranks)
    )
    inputs_own = tokens.astype(jnp.float32)
    normed, unit_first, inverse_first = norm_forward(
        inputs_own + attention + out_biases[0], ln_gains[0], ln_shifts[0]
    )
    normed_low = normed.astype(low)

    def activate(up, up_bias):
        hidden = jnp.dot(normed_low, up, preferred_element_type=jnp.float32) + up_bias
        below = 0.5 * (1.0 + lax.erf(hidden * ROOT_HALF))
        density = jnp.exp(-0.5 * hidden * hidden) * GAUSS_NORM
        return meet((hidden * below).astype(low), (below + hidden * density).astype(low))

    normed_low, up_corner, down_second, down_third = meet(
        normed_low, up_corner, down_second, down_third
    )
    up_half = joined([up_first, up_second, up_third, *up_corner])
    up_far = send(up_half, 1)
    down_corner = corner(down_second, down_third)
    pairs_active = [activate(up_own, up_bias)]
    pairs_active, up_far = meet(pairs_active, up_far)
    ups = [up_own] + [
        spread(near, far, place, 2, low) for near, far in zip(up_half, up_far, strict=True)
    ]
    ups, down_corner = meet(ups, down_corner)
    down_half = joined([down_first, down_second, down_third, *down_corner])
    down_far = send(down_half, 1)
    pairs_active += [activate(ups[k], up_biases[k]) for k in others]
    pairs_active, down_far = meet(pairs_active, down_far)
    downs = [down_own] + [
        spread(near, far, place, 2, low) for near, far in zip(down_half, down_far, strict=True)
    ]
    active, slope = zip(*pairs_active, strict=True)
    branch = 0.0
    for k in range(ranks):
        branch = branch + jnp.dot(active[k], downs[k], preferred_element_type=jnp.float32)
    result, unit_second, inverse_second = norm_forward(
        normed + branch + out_biases[1], ln_gains[1], ln_shifts[1]
    )

    out_grad = cotangent.astype(jnp.float32) * (docs[0] < DOCS_DEV).astype(jnp.float32)[:, None]
    second_grad, gain_grad_second, shift_grad_second = norm_backward(
        out_grad, unit_second, inverse_second, ln_gains[1]
    )
    bias_grad_second = jnp.sum(second_grad, axis=0)
    branch_grad = second_grad.astype(low)
    down_parts = [
        jnp.einsum("sf,sd->fd", active[k], branch_grad, preferred_element_type=jnp.float32).astype(
            low
        )
        for k in range(ranks)
    ]
    down_parts, branch_grad = meet(down_parts, branch_grad)
    down_away, down_keep = opening(down_parts, dp_pos, masks[0])
    down_away, branch_grad = meet(down_away, branch_grad)
    down_got = send(down_away, masks[0])
    hidden_grads = []
    for k in range(ranks):
        active_grad = jnp.einsum(
            "sd,fd->sf", branch_grad, downs[k], preferred_element_type=jnp.float32
        )
        hidden_grads.append((active_grad * slope[k].astype(jnp.float32)).astype(low))
    hidden_grads, down_got = meet(hidden_grads, down_got)
    down_away, down_keep = fold(down_keep, down_got, dp_pos, masks[1])
    down_away, hidden_grads = meet(down_away, hidden_grads)
    down_got = send(down_away, masks[1])
    up_parts = [
        jnp.einsum(
            "sd,sf->df", normed_low, hidden_grads[k], preferred_element_type=jnp.float32
        ).astype(low)
        for k in range(ranks)
    ]
    up_away, up_keep = opening(up_parts, dp_pos, masks_up[0])
    up_away, hidden_grads = meet(up_away, hidden_grads)
    up_got = send(up_away, masks_up[0])
    normed_grad = second_grad
    for k in range(ranks):
        normed_grad = normed_grad + jnp.einsum(
            "sf,df->sd", hidden_grads[k], ups[k], preferred_element_type=jnp.float32
        )
    first_grad, gain_grad_first, shift_grad_first = norm_backward(
        normed_grad, unit_first, inverse_first, ln_gains[0]
    )
    bias_grad_first = jnp.sum(first_grad, axis=0)
    attn_grad = first_grad.astype(low)
    mixed_grads = [
        jnp.einsum("sd,cd->sc", attn_grad, outs[k], preferred_element_type=jnp.float32).astype(low)
        for k in range(ranks)
    ]
    mixed_grads, up_got = meet(mixed_grads, up_got)
    grads_got = exchange(mixed_grads)
    up_away, up_keep = fold(up_keep, up_got, dp_pos, masks_up[1])
    up_got = send(up_away, masks_up[1])
    out_parts = [
        jnp.einsum("sc,sd->cd", mixed_got[k], attn_grad, preferred_element_type=jnp.float32).astype(
            low
        )
        for k in range(ranks)
    ]
    out_away, out_keep = opening(out_parts, dp_pos, masks[0])
    out_away, grads_got = meet(out_away, grads_got[1:])
    out_got = send(out_away, masks[0])
    grads_rest = grads_got[0] if ranks == 2 else jnp.concatenate(grads_got, axis=0)
    block = min(256, rows_own)
    qkv_grads = attn_backward(
        qkv_own, qkv_rest, mixed_grads[0], grads_rest, mixed, lse, seen, bar, scale, block, 0, early
    )
    qkv_grads, down_got, out_got = meet(qkv_grads, down_got, out_got)
    down_keep, down_got = fold_ranks(down_keep, down_got)
    out_away, out_keep = fold(out_keep, out_got, dp_pos, masks[1])
    out_got = send(out_away, masks[1])
    if pairs > early:
        qkv_grads = attn_backward(
            qkv_own,
            qkv_rest,
            mixed_grads[0],
            grads_rest,
            mixed,
            lse,
            seen,
            bar,
            scale,
            block,
            early,
            pairs - early,
            tuple(qkv_grads),
        )
    qkv_grads, down_got, up_got, out_got = meet(qkv_grads, down_got, up_got, out_got)
    down_sum = add_ranks(down_keep, down_got)
    down_away, down_keep = opening([down_sum], dp_pos, masks[2])
    down_got = send(down_away, masks[2])
    up_keep, up_got = fold_ranks(up_keep, up_got)
    out_keep, out_got = fold_ranks(out_keep, out_got)
    qkv_grad_own, qkv_grad_rest = qkv_grads

    def input_part(item):
        return jnp.einsum("isc,idc->sd", item, w_qkv, preferred_element_type=jnp.float32)

    grad_qkv = jnp.einsum("sd,isc->idc", rest, qkv_grad_rest, preferred_element_type=jnp.float32)
    grad_qkv = grad_qkv + jnp.einsum(
        "sd,isc->idc", tokens, qkv_grad_own, preferred_element_type=jnp.float32
    )
    qkv_away, qkv_keep = opening([grad_qkv.astype(low).reshape(3 * D, width)], dp_pos, masks[0])
    qkv_got = send(qkv_away, masks[0])
    far = input_part(qkv_grad_rest).astype(low)
    far, qkv_got, down_got = meet(far, qkv_got, down_got)
    qkv_away, qkv_keep = fold(qkv_keep, qkv_got, dp_pos, masks[1])
    qkv_got = send(qkv_away, masks[1])
    down_sum = scatter_on(add(down_keep, down_got)[0], dp_pos, masks[3:])
    near = input_part(qkv_grad_own)
    near, up_got, far = meet(near, up_got, far)
    inputs_got = exchange(
        [None] + [far[k * rows_own : (k + 1) * rows_own] for k in range(ranks - 1)]
    )
    up_sum = scatter_on(add_ranks(up_keep, up_got), dp_pos, masks_up[2:])
    qkv_sum = scatter_on(add(qkv_keep, qkv_got)[0], dp_pos, masks[2:])
    grad_down = gather_rows(down_sum, dp_pos, masks)
    grad_up = gather_rows(up_sum, dp_pos, masks_up)
    grad_qkv = gather_rows(qkv_sum, dp_pos, masks)
    out_sum = add_ranks(out_keep, out_got)
    if (out_sum.shape[0] * 4 // count_dp) % 16 == 0:
        grad_out = gather_rows(scatter_on(out_sum, dp_pos, masks[2:]), dp_pos, masks)
    else:
        for mask in masks[2:]:
            out_sum = add([out_sum], send([out_sum], mask))[0]
        half = jnp.concatenate([out_sum, xor_step(out_sum, masks[1])], axis=0)
        grad_out = spread(half, xor_step(half, masks[0]), out_place, 1, jnp.float32)

    up_sums = [jnp.sum(item.astype(jnp.float32), axis=0) for item in hidden_grads]
    sums_got = exchange(up_sums)
    hidden_sum = up_sums[0]
    for piece in sums_got[1:]:
        hidden_sum = hidden_sum + piece
    shared = butterfly(
        jnp.stack(
            [
                bias_grad_first,
                bias_grad_second,
                gain_grad_first,
                gain_grad_second,
                shift_grad_first,
                shift_grad_second,
            ]
        ),
        "tensor",
    )
    shared = butterfly(jnp.concatenate([shared.reshape(-1), hidden_sum]), "dp")
    shared, grad_up_bias = shared[: 6 * D].reshape(6, D), shared[6 * D :]
    qkv_sums = jnp.sum(qkv_grad_own.astype(jnp.float32), axis=1) + jnp.sum(
        qkv_grad_rest.astype(jnp.float32), axis=1
    )
    grad_qv = butterfly(jnp.stack([qkv_sums[0], qkv_sums[2]]), "dp")
    grad_input = first_grad + near
    for piece in inputs_got[1:]:
        grad_input = grad_input + piece.astype(jnp.float32)
    return (
        result.astype(low),
        grad_input.astype(low),
        grad_qkv.reshape(3, D, width),
        grad_qv,
        grad_out,
        shared[0:2],
        shared[2:4],
        shared[4:6],
        grad_up,
        grad_up_bias,
        grad_down,
    )


def solution(mesh):
    placed = (
        P(("dp", "tensor"), None),
        P("dp"),
        P(None, None, "tensor"),
        P(None, "tensor"),
        P("tensor", None),
        P(),
        P(),
        P(),
        P(None, "tensor"),
        P("tensor"),
        P("tensor", None),
        P(("dp", "tensor"), None),
    )
    return jax.shard_map(
        shards,
        mesh=mesh,
        in_specs=placed,
        out_specs=(
            P(("dp", "tensor"), None),
            P(("dp", "tensor"), None),
            P(None, None, "tensor"),
            P(None, "tensor"),
            P("tensor", None),
            P(),
            P(),
            P(),
            P(None, "tensor"),
            P("tensor"),
            P("tensor", None),
        ),
        check_vma=False,
    )
```

```python
import functools
import math

import jax
import jax.numpy as jnp
from jax import lax
from jax.experimental import pallas as pl
from jax.experimental.pallas import tpu as pltpu
from jax.sharding import PartitionSpec as P

D = 1024
H = 16
DOCS_DEV = 4


EPSILON = 1e-06
ROOT_HALF = 0.7071067811865476
GAUSS_NORM = 0.3989422804014327
NT = (((1,), (1,)), ((), ()))
VMEM_ASK = 48 << 20


def norm_forward(summed, gain, shift):
    centred = summed - jnp.mean(summed, axis=-1, keepdims=True)
    inverse = lax.rsqrt(jnp.mean(centred * centred, axis=-1, keepdims=True) + EPSILON)
    unit = centred * inverse
    return (unit * gain + shift, unit, inverse)


def norm_backward(upstream, unit, inverse, gain):
    spread = upstream * gain
    inner = (
        spread
        - jnp.mean(spread, axis=-1, keepdims=True)
        - unit * jnp.mean(spread * unit, axis=-1, keepdims=True)
    )
    return (inner * inverse, jnp.sum(upstream * unit, axis=0), jnp.sum(upstream, axis=0))


def attn_forward_kernel(block, scale, own_ref, rest_ref, seen_ref, bar_ref, *refs):
    mixed_ref, lse_ref = refs[-2:]
    lane = lax.broadcasted_iota(jnp.int32, (1, 128), 1)
    rows = own_ref.shape[1] + rest_ref.shape[1]
    keys = jnp.concatenate([own_ref[1], rest_ref[1]], axis=0)
    values_t = jnp.concatenate([own_ref[2], rest_ref[2]], axis=0).T
    queries = jnp.concatenate([own_ref[0], rest_ref[0]], axis=0) * jnp.bfloat16(scale)
    half = [(lane // 64) == h for h in range(2)]
    keys_of = [jnp.where(half[h], keys, bar_ref[...]) for h in range(2)]
    for first in range(0, rows, block):
        span = slice(first, first + block)
        out_t = []
        for h in range(2):
            query = jnp.where(half[h], queries[span], seen_ref[span])
            scores = lax.dot_general(keys_of[h], query, NT, preferred_element_type=jnp.float32)
            top = jnp.max(scores, axis=0, keepdims=True)
            expd = jnp.exp(scores - top)
            total = jnp.sum(expd, axis=0, keepdims=True)
            mixed = jnp.dot(
                values_t[64 * h : 64 * h + 64],
                expd.astype(jnp.bfloat16),
                preferred_element_type=jnp.float32,
            )
            out_t.append(mixed / total)
            lse_ref[0, h : h + 1, span] = top + jnp.log(total)
        mixed_ref[span] = jnp.concatenate(out_t, axis=0).T.astype(jnp.bfloat16)


def attn_backward_kernel(
    block,
    scale,
    own_ref,
    rest_ref,
    up_own_ref,
    up_rest_ref,
    mixed_ref,
    lse_ref,
    seen_ref,
    bar_ref,
    grad_own_ref,
    grad_rest_ref,
    key_acc,
    value_acc,
):
    lane = lax.broadcasted_iota(jnp.int32, (1, 128), 1)
    rows_own = own_ref.shape[1]
    rows = rows_own + rest_ref.shape[1]
    keys = jnp.concatenate([own_ref[1], rest_ref[1]], axis=0)
    values = jnp.concatenate([own_ref[2], rest_ref[2]], axis=0)
    keys_t = keys.T
    half = [(lane // 64) == h for h in range(2)]
    keys_of = [jnp.where(half[h], keys, bar_ref[...]) for h in range(2)]
    nothing = jnp.zeros((block, 128), jnp.bfloat16)
    for first in range(0, rows, block):
        span = slice(first, first + block)
        if first < rows_own:
            here, source, up_ref, out_ref = span, own_ref, up_own_ref, grad_own_ref
        else:
            here = slice(first - rows_own, first - rows_own + block)
            source, up_ref, out_ref = rest_ref, up_rest_ref, grad_rest_ref
        query_rows = source[0, here]
        up_rows = up_ref[here]
        product = (up_rows.astype(jnp.float32) * mixed_ref[span].astype(jnp.float32)).T
        query_grad_t = []
        for h in range(2):
            query = jnp.where(half[h], query_rows * jnp.bfloat16(scale), seen_ref[span])
            up = jnp.where(half[h], up_rows, nothing)
            scores = lax.dot_general(keys_of[h], query, NT, preferred_element_type=jnp.float32)
            probs = jnp.exp(scores - lse_ref[0, h : h + 1, span])
            spread = lax.dot_general(values, up, NT, preferred_element_type=jnp.float32)
            inner = jnp.sum(product[64 * h : 64 * h + 64], axis=0, keepdims=True)
            score_grad = (probs * (spread - inner)).astype(jnp.bfloat16)
            value_part = jnp.dot(probs.astype(jnp.bfloat16), up, preferred_element_type=jnp.float32)
            key_part = jnp.dot(
                score_grad, jnp.where(half[h], query_rows, nothing), preferred_element_type=jnp.float32
            )
            if first == 0 and h == 0:
                value_acc[...] = value_part
                key_acc[...] = key_part
            else:
                value_acc[...] += value_part
                key_acc[...] += key_part
            query_grad_t.append(
                jnp.dot(keys_t[64 * h : 64 * h + 64], score_grad, preferred_element_type=jnp.float32)
            )
        out_ref[0, here] = (jnp.concatenate(query_grad_t, axis=0).T * scale).astype(jnp.bfloat16)
    key_low = (key_acc[...] * scale).astype(jnp.bfloat16)
    value_low = value_acc[...].astype(jnp.bfloat16)
    grad_own_ref[1] = key_low[:rows_own]
    grad_rest_ref[1] = key_low[rows_own:]
    grad_own_ref[2] = value_low[:rows_own]
    grad_rest_ref[2] = value_low[rows_own:]


def attn_forward(own, rest, seen, bar, scale, block, start, count, previous=()):
    rows_own, rows_rest, width = own.shape[1], rest.shape[1], own.shape[2]
    rows = rows_own + rows_rest
    return pl.pallas_call(
        functools.partial(attn_forward_kernel, block, scale),
        grid=(count,),
        in_specs=[
            pl.BlockSpec((3, rows_own, 128), lambda p: (0, 0, p + start)),
            pl.BlockSpec((3, rows_rest, 128), lambda p: (0, 0, p + start)),
            pl.BlockSpec((rows, 128), lambda p: (0, 0)),
            pl.BlockSpec((rows, 128), lambda p: (0, 0)),
        ]
        + [pl.BlockSpec(memory_space=pl.ANY)] * len(previous),
        out_specs=[
            pl.BlockSpec((rows, 128), lambda p: (0, p + start)),
            pl.BlockSpec((1, 8, rows), lambda p: (p + start, 0, 0)),
        ],
        out_shape=[
            jax.ShapeDtypeStruct((rows, width), jnp.bfloat16),
            jax.ShapeDtypeStruct((width // 128, 8, rows), jnp.float32),
        ],
        input_output_aliases={4: 0, 5: 1} if previous else {},
        compiler_params=pltpu.CompilerParams(vmem_limit_bytes=VMEM_ASK),
        cost_estimate=pl.CostEstimate(
            flops=count * rows * rows, transcendentals=0, bytes_accessed=count * rows
        ),
        name="attn_forward",
    )(own, rest, seen, bar, *previous)


def attn_backward(own, rest, up_own, up_rest, mixed, lse, seen, bar, scale, block, start, count):
    rows_own, rows_rest = own.shape[1], rest.shape[1]
    rows = rows_own + rows_rest
    return pl.pallas_call(
        functools.partial(attn_backward_kernel, block, scale),
        grid=(count,),
        in_specs=[
            pl.BlockSpec((3, rows_own, 128), lambda p: (0, 0, p + start)),
            pl.BlockSpec((3, rows_rest, 128), lambda p: (0, 0, p + start)),
            pl.BlockSpec((rows_own, 128), lambda p: (0, p + start)),
            pl.BlockSpec((rows_rest, 128), lambda p: (0, p + start)),
            pl.BlockSpec((rows, 128), lambda p: (0, p + start)),
            pl.BlockSpec((1, 8, rows), lambda p: (p + start, 0, 0)),
            pl.BlockSpec((rows, 128), lambda p: (0, 0)),
            pl.BlockSpec((rows, 128), lambda p: (0, 0)),
        ],
        out_specs=[
            pl.BlockSpec((3, rows_own, 128), lambda p: (0, 0, p)),
            pl.BlockSpec((3, rows_rest, 128), lambda p: (0, 0, p)),
        ],
        out_shape=[
            jax.ShapeDtypeStruct((3, rows_own, count * 128), jnp.bfloat16),
            jax.ShapeDtypeStruct((3, rows_rest, count * 128), jnp.bfloat16),
        ],
        scratch_shapes=[pltpu.VMEM((rows, 128), jnp.float32)] * 2,
        compiler_params=pltpu.CompilerParams(vmem_limit_bytes=VMEM_ASK),
        cost_estimate=pl.CostEstimate(
            flops=count * rows * rows, transcendentals=0, bytes_accessed=count * rows
        ),
        name="attn_backward",
    )(own, rest, up_own, up_rest, mixed, lse, seen, bar)


def doc_features(docs):
    slot = lax.broadcasted_iota(jnp.int32, (1, 128), 1) % 64
    same = docs[:, None] == slot
    seen = same.astype(jnp.bfloat16)
    bar = jnp.where(same | (slot > 4), 0.0, -(2.0**30)).astype(jnp.bfloat16)
    return seen, bar


def xor_step(array, mask):
    size = lax.axis_size("dp")
    return lax.ppermute(array, "dp", [(i, i ^ mask) for i in range(size)])


def from_rank(array, ahead):
    size = lax.axis_size("tensor")
    return lax.ppermute(array, "tensor", [((i + ahead) % size, i) for i in range(size)])


def exchange(parts):
    size = lax.axis_size("tensor")
    got = [None] * size
    for ahead in range(1, size):
        got[size - ahead] = lax.ppermute(
            parts[ahead], "tensor", [(i, (i + ahead) % size) for i in range(size)]
        )
    return got


def meet(*trees):
    return lax.optimization_barrier(trees)


def spread_kernel(count, order_ref, near_ref, far_ref, *refs):
    out_ref = refs[-1]
    step = pl.program_id(0)
    rows = near_ref.shape[1] // count

    def store(ref):
        for index in range(count):
            offset = pl.multiple_of(order_ref[4 + index] * rows, rows)
            out_ref[:, pl.ds(offset, rows)] = ref[:, index * rows : (index + 1) * rows].astype(
                out_ref.dtype
            )

    @pl.when(step < 2)
    def _():
        store(near_ref)

    @pl.when(step > 1)
    def _():
        store(far_ref)


def spread(near, far, place, count, kind, column=0, columns_all=None, previous=()):
    lead, rows, columns = near.shape[0], near.shape[1] // 2, near.shape[2]
    quarter, inner = lax.div(place, jnp.int32(count)), lax.rem(place, jnp.int32(count))
    order = jnp.concatenate(
        [
            jnp.bitwise_xor(quarter, jnp.arange(4, dtype=jnp.int32)),
            jnp.bitwise_xor(inner, jnp.arange(count, dtype=jnp.int32)),
        ]
    )
    block = (lead, rows, columns)
    return pl.pallas_call(
        functools.partial(spread_kernel, count),
        grid_spec=pltpu.PrefetchScalarGridSpec(
            num_scalar_prefetch=1,
            grid=(4,),
            in_specs=[
                pl.BlockSpec(block, lambda step, order: (0, jnp.minimum(step, 1), 0)),
                pl.BlockSpec(block, lambda step, order: (0, jnp.maximum(step - 2, 0), 0)),
            ]
            + [pl.BlockSpec(memory_space=pl.ANY)] * len(previous),
            out_specs=pl.BlockSpec(block, lambda step, order: (0, order[step], column)),
        ),
        out_shape=jax.ShapeDtypeStruct((lead, 4 * rows, columns_all or columns), kind),
        input_output_aliases={3: 0} if previous else {},
        compiler_params=pltpu.CompilerParams(vmem_limit_bytes=VMEM_ASK // 2),
        cost_estimate=pl.CostEstimate(
            flops=0, transcendentals=0, bytes_accessed=24 * lead * rows * columns
        ),
        name="spread_rows",
    )(order, near, far, *previous)


def bit_of(dp_pos, mask):
    return jnp.where(lax.bitwise_and(dp_pos, mask) != 0, 1, 0).astype(jnp.int32)


def half_of(array, index):
    rows = array.shape[1] // 2
    return lax.dynamic_slice_in_dim(array, index * rows, rows, 1)


def opening(parts, dp_pos, mask):
    bit = bit_of(dp_pos, mask)
    return [half_of(part, 1 - bit) for part in parts], [half_of(part, bit) for part in parts]


def send(arrays, mask):
    return [xor_step(array, mask) for array in arrays]


def add(keep, got):
    return [
        (a.astype(jnp.float32) + b.astype(jnp.float32)).astype(a.dtype)
        for a, b in zip(keep, got, strict=True)
    ]


def fold(keep, got, dp_pos, mask):
    bit = bit_of(dp_pos, mask)
    away = add([half_of(a, 1 - bit) for a in keep], [half_of(b, 1 - bit) for b in got])
    kept = add([half_of(a, bit) for a in keep], [half_of(b, bit) for b in got])
    return away, kept


def fold_ranks(keep, got):
    total = add(keep, got)
    return [total[0]], exchange(total)[1:]


def add_ranks(keep, got):
    total = keep[0].astype(jnp.float32)
    for piece in got:
        total = total + piece.astype(jnp.float32)
    return total.astype(keep[0].dtype)


def scatter_on(array, dp_pos, masks):
    for mask in masks:
        away, keep = opening([array], dp_pos, mask)
        array = add(keep, send(away, mask))[0]
    return array


def gather_rows(mine, dp_pos, masks, *where):
    for mask in reversed(masks[1:]):
        mine = jnp.concatenate([mine, xor_step(mine, mask)], axis=1)
    place = jnp.int32(0)
    for mask in masks:
        place = 2 * place + bit_of(dp_pos, mask)
    far = xor_step(mine, masks[0])
    return spread(mine, far, place, 2 ** (len(masks) - 2), jnp.float32, *where)


def butterfly(array, axis):
    size = lax.axis_size(axis)
    mask = 1
    while mask < size:
        array = array + lax.ppermute(array, axis, [(i, i ^ mask) for i in range(size)])
        mask *= 2
    return array


def shards(
    tokens,
    doc_ids,
    w_qkv,
    qv_bias,
    out_weight,
    out_biases,
    ln_gains,
    ln_shifts,
    up_weight,
    up_bias,
    down_weight,
    cotangent,
):
    low = jnp.bfloat16
    rows_own = tokens.shape[0]
    ranks = lax.axis_size("tensor")
    tensor_pos = lax.axis_index("tensor")
    dp_pos = lax.axis_index("dp")
    head_size = D // H
    width = w_qkv.shape[2]
    scale = 1.0 / math.sqrt(head_size)

    count_dp = lax.axis_size("dp")
    masks = [2**k for k in range(count_dp.bit_length() - 1)]
    masks_up = [masks[0], masks[2], masks[1]] + masks[3:]
    others = range(1, ranks)
    same_core = [[i for i in range(count_dp) if i % 2 == side] for side in range(2)]

    rest = [from_rank(tokens, ahead) for ahead in others]
    rest = rest[0] if ranks == 2 else jnp.concatenate(rest, axis=0)
    up_biases = [up_bias] + [from_rank(up_bias, ahead) for ahead in others]
    out_own, up_own, down_own, rest = meet(out_weight, up_weight, down_weight, rest)

    place = 4 * bit_of(dp_pos, 1) + 2 * bit_of(dp_pos, 4) + bit_of(dp_pos, 2)

    def slice_from(weight, pieces, index):
        rows = weight.shape[0] // pieces
        mine = lax.dynamic_slice_in_dim(weight, index * rows, rows, 0)
        return [from_rank(mine, ahead) for ahead in others]

    def joined(groups):
        return [jnp.concatenate(items, axis=0) for items in zip(*groups, strict=True)]

    def corner(by_first, by_second):
        rows = by_first[0].shape[0] // 2
        return (
            [xor_step(item[:rows], 2) for item in by_second],
            [xor_step(item[rows:], 4) for item in by_first],
        )

    out_place = 2 * bit_of(dp_pos, 1) + bit_of(dp_pos, 2)
    out_first, up_first = slice_from(out_own, 4, out_place), slice_from(up_own, 8, place)
    docs = [
        lax.dynamic_slice_in_dim(
            doc_ids, lax.rem(tensor_pos + ahead, ranks) * rows_own, rows_own, 0
        )
        for ahead in range(ranks)
    ]
    seen, bar = doc_features(jnp.concatenate(docs, axis=0))
    bias = jnp.stack([qv_bias[0], jnp.zeros_like(qv_bias[0]), qv_bias[1]])[:, None, :]

    def project(rows):
        wide = jnp.einsum("sd,idc->isc", rows, w_qkv, preferred_element_type=jnp.float32)
        return (wide + bias).astype(low)

    qkv_own, qkv_rest = project(tokens), project(rest)
    qkv_rest, down_own, out_first = meet(qkv_rest, down_own, out_first)
    down_first = slice_from(down_own, 8, place)
    out_second = send(out_first, 2)
    pairs = width // 128
    early = max(1, pairs // 2)
    block = min(512, rows_own)
    mixed_lse = attn_forward(qkv_own, qkv_rest, seen, bar, scale, block, 0, early)
    mixed_lse, out_second, up_first = meet(mixed_lse, out_second, up_first)
    up_second, up_third = send(up_first, 2), send(up_first, 4)
    if pairs > early:
        mixed_lse = attn_forward(
            qkv_own, qkv_rest, seen, bar, scale, block, early, pairs - early, tuple(mixed_lse)
        )
    out_half = joined([out_first, out_second])
    out_far = send(out_half, 1)
    mixed_lse, down_first = meet(mixed_lse, down_first)
    down_second, down_third = send(down_first, 2), send(down_first, 4)
    mixed, lse = mixed_lse
    mixed_parts = [mixed[k * rows_own : (k + 1) * rows_own] for k in range(ranks)]
    mixed_got = exchange(mixed_parts)
    mixed_got[0] = mixed_parts[0]
    mixed_got, out_far, up_second, up_third, up_biases = meet(
        mixed_got, out_far, up_second, up_third, up_biases
    )
    up_corner = corner(up_second, up_third)
    outs = [out_own] + [
        spread(near[None], far[None], out_place, 1, low)[0] for near, far in zip(out_half, out_far, strict=True)
    ]
    attention = sum(
        jnp.dot(mixed_got[k], outs[k], preferred_element_type=jnp.float32) for k in range(ranks)
    )
    inputs_own = tokens.astype(jnp.float32)
    normed, unit_first, inverse_first = norm_forward(
        inputs_own + attention + out_biases[0], ln_gains[0], ln_shifts[0]
    )
    normed_low = normed.astype(low)

    def activate(up, up_bias):
        hidden = jnp.dot(normed_low, up, preferred_element_type=jnp.float32) + up_bias
        below = 0.5 * (1.0 + lax.erf(hidden * ROOT_HALF))
        density = jnp.exp(-0.5 * hidden * hidden) * GAUSS_NORM
        return meet((hidden * below).astype(low), (below + hidden * density).astype(low))

    pairs_active = [activate(up_own, up_bias)]
    pairs_active, up_corner, down_second, down_third = meet(
        pairs_active, up_corner, down_second, down_third
    )
    up_half = joined([up_first, up_second, up_third, *up_corner])
    up_far = send(up_half, 1)
    down_corner = corner(down_second, down_third)
    branch = jnp.dot(pairs_active[0][0], down_own, preferred_element_type=jnp.float32)
    branch, up_far, down_corner = meet(branch, up_far, down_corner)
    down_half = joined([down_first, down_second, down_third, *down_corner])
    down_far = send(down_half, 1)
    ups = [up_own] + [
        spread(near[None], far[None], place, 2, low)[0]
        for near, far in zip(up_half, up_far, strict=True)
    ]
    pairs_active += [activate(ups[k], up_biases[k]) for k in others]
    pairs_active, down_far = meet(pairs_active, down_far)
    downs = [down_own] + [
        spread(near[None], far[None], place, 2, low)[0]
        for near, far in zip(down_half, down_far, strict=True)
    ]
    active, slope = zip(*pairs_active, strict=True)
    for k in others:
        branch = branch + jnp.dot(active[k], downs[k], preferred_element_type=jnp.float32)
    result, unit_second, inverse_second = norm_forward(
        normed + branch + out_biases[1], ln_gains[1], ln_shifts[1]
    )

    out_grad = cotangent.astype(jnp.float32) * (docs[0] < DOCS_DEV).astype(jnp.float32)[:, None]
    second_grad, gain_grad_second, shift_grad_second = norm_backward(
        out_grad, unit_second, inverse_second, ln_gains[1]
    )
    bias_grad_second = jnp.sum(second_grad, axis=0)
    branch_grad = second_grad.astype(low)
    down_parts = [
        jnp.einsum("sf,sd->fd", active[k], branch_grad, preferred_element_type=jnp.float32).astype(
            low
        )
        for k in range(ranks)
    ]
    down_parts, branch_grad = meet(down_parts, branch_grad)
    down_away, down_keep = opening([part[None] for part in down_parts], dp_pos, masks[0])
    down_away, branch_grad = meet(down_away, branch_grad)
    down_got = send(down_away, masks[0])
    hidden_grads = []
    for k in range(ranks):
        active_grad = jnp.einsum(
            "sd,fd->sf", branch_grad, downs[k], preferred_element_type=jnp.float32
        )
        hidden_grads.append((active_grad * slope[k].astype(jnp.float32)).astype(low))
    hidden_grads, down_got = meet(hidden_grads, down_got)
    down_sums = add(down_keep, down_got)
    down_sums, hidden_grads = meet(down_sums, hidden_grads)
    down_got = exchange(down_sums)[1:]
    normed_grad = second_grad
    for k in range(ranks):
        normed_grad = normed_grad + jnp.einsum(
            "sf,df->sd", hidden_grads[k], ups[k], preferred_element_type=jnp.float32
        )
    first_grad, gain_grad_first, shift_grad_first = norm_backward(
        normed_grad, unit_first, inverse_first, ln_gains[0]
    )
    bias_grad_first = jnp.sum(first_grad, axis=0)
    attn_grad = first_grad.astype(low)
    mixed_grads = [
        jnp.einsum("sd,cd->sc", attn_grad, outs[k], preferred_element_type=jnp.float32).astype(low)
        for k in range(ranks)
    ]
    grads_got = exchange(mixed_grads)[1:]
    up_parts = [
        jnp.einsum(
            "sd,sf->df", normed_low, hidden_grads[k], preferred_element_type=jnp.float32
        ).astype(low)
        for k in range(ranks)
    ]
    up_away, up_keep = opening([part[None] for part in up_parts], dp_pos, masks_up[0])
    up_got = send(up_away, masks_up[0])
    out_parts = [
        jnp.einsum("sc,sd->cd", mixed_got[k], attn_grad, preferred_element_type=jnp.float32).astype(
            low
        )
        for k in range(ranks)
    ]

    out_away, out_keep = opening([part[None] for part in out_parts], dp_pos, masks[0])
    out_away, up_got, grads_got = meet(out_away, up_got, grads_got)
    out_got = send(out_away, masks[0])
    up_away, up_keep = fold(up_keep, up_got, dp_pos, masks_up[1])
    up_away, mixed_grads, grads_got = meet(up_away, mixed_grads, grads_got)
    up_got = send(up_away, masks_up[1])
    grads_rest = grads_got[0] if ranks == 2 else jnp.concatenate(grads_got, axis=0)
    block = min(256, rows_own)

    def backward(start, count):
        return attn_backward(
            qkv_own,
            qkv_rest,
            mixed_grads[0],
            grads_rest,
            mixed,
            lse,
            seen,
            bar,
            scale,
            block,
            start,
            count,
        )

    def open_qkv(chunk):
        own, far = chunk
        total = jnp.einsum("sd,isc->idc", rest, far, preferred_element_type=jnp.float32)
        total = total + jnp.einsum("sd,isc->idc", tokens, own, preferred_element_type=jnp.float32)
        return opening([total.astype(low)], dp_pos, masks[0])

    chunks = [backward(0, early)]
    chunks, out_got = meet(chunks, out_got)
    out_keep, out_got = fold_ranks(out_keep, out_got)
    qkv_away, qkv_keep = open_qkv(chunks[0])
    qkv_state = [(qkv_keep, send(qkv_away, masks[0]))]
    if pairs > early:
        chunks, qkv_away, grads_rest = meet(chunks, qkv_away, grads_rest)
        chunks = [chunks[0], backward(early, pairs - early)]
        chunks, qkv_state = meet(chunks, qkv_state)
        keep, got = qkv_state[0]
        qkv_away, qkv_keep = fold(keep, got, dp_pos, masks[1])
        qkv_state = [(qkv_keep, send(qkv_away, masks[1]))]
        qkv_away, qkv_keep = open_qkv(chunks[1])
        qkv_away, down_got, out_got = meet(qkv_away, down_got, out_got)
        halves = lax.psum(
            (add_ranks([down_sums[0]], down_got), add_ranks(out_keep, out_got)),
            "dp",
            axis_index_groups=same_core,
        )
        qkv_state.append((qkv_keep, send(qkv_away, masks_up[0])))
    else:
        halves = lax.psum(
            (add_ranks([down_sums[0]], down_got), add_ranks(out_keep, out_got)),
            "dp",
            axis_index_groups=same_core,
        )
        keep, got = qkv_state[0]
        qkv_away, qkv_keep = fold(keep, got, dp_pos, masks[1])
        qkv_state = [(qkv_keep, send(qkv_away, masks[1]))]
    up_keep, up_got = fold_ranks(up_keep, up_got)

    edges = [0, early * 128, width]

    def input_part(side):
        total = 0.0
        for index, chunk in enumerate(chunks):
            total = total + jnp.einsum(
                "isc,idc->sd",
                chunk[side],
                w_qkv[:, :, edges[index] : edges[index + 1]],
                preferred_element_type=jnp.float32,
            )
        return total

    if pairs > early:
        keep, got = qkv_state[1]
        qkv_away, qkv_keep = fold(keep, got, dp_pos, masks_up[1])
        qkv_state[1] = (qkv_keep, send(qkv_away, masks_up[1]))
    far = input_part(1).astype(low)
    near = input_part(0)
    near, up_got, far = meet(near, up_got, far)
    inputs_got = exchange(
        [None] + [far[k * rows_own : (k + 1) * rows_own] for k in range(ranks - 1)]
    )
    up_sum = scatter_on(add_ranks(up_keep, up_got), dp_pos, masks_up[2:])
    orders = [masks, masks_up]
    qkv_sums = [
        scatter_on(add(*state)[0], dp_pos, order[2:])
        for state, order in zip(qkv_state, orders[: len(chunks)], strict=True)
    ]
    grad_up = gather_rows(up_sum, dp_pos, masks_up)[0]
    grad_qkv = gather_rows(qkv_sums[0], dp_pos, masks, 0, width)
    if pairs > early:
        grad_qkv = gather_rows(qkv_sums[1], dp_pos, masks_up, 1, width, (grad_qkv,))
    halves, grad_qkv, grad_up = meet(halves, grad_qkv, grad_up)
    core_place = 2 * bit_of(dp_pos, masks[0])
    grad_down, grad_out = [
        spread(half, xor_step(half, masks[0]), core_place, 1, jnp.float32)[0] for half in halves
    ]
    column_sums = jnp.concatenate(
        [
            jnp.sum(own.astype(jnp.float32), axis=1) + jnp.sum(far.astype(jnp.float32), axis=1)
            for own, far in chunks
        ],
        axis=1,
    )
    hidden_sums = [jnp.sum(item.astype(jnp.float32), axis=0) for item in hidden_grads]
    shared = jnp.concatenate(
        [
            bias_grad_first,
            bias_grad_second,
            gain_grad_first,
            gain_grad_second,
            shift_grad_first,
            shift_grad_second,
        ]
    )
    shared, hidden_sums, chunks = meet(shared, hidden_sums, chunks)
    shared = butterfly(shared, "tensor")
    hidden_sum = hidden_sums[0]
    for piece in exchange(hidden_sums)[1:]:
        hidden_sum = hidden_sum + piece
    cuts = [6 * D, 6 * D + hidden_sum.shape[0], 6 * D + hidden_sum.shape[0] + width]
    sums = butterfly(
        jnp.concatenate([shared, hidden_sum, column_sums[0], column_sums[2]]), "dp"
    )
    shared, grad_up_bias = sums[: cuts[0]].reshape(6, D), sums[cuts[0] : cuts[1]]
    grad_qv = sums[cuts[1] :].reshape(2, width)
    grad_input = first_grad + near
    for piece in inputs_got[1:]:
        grad_input = grad_input + piece.astype(jnp.float32)
    return (
        result.astype(low),
        grad_input.astype(low),
        grad_qkv.reshape(3, D, width),
        grad_qv,
        grad_out,
        shared[0:2],
        shared[2:4],
        shared[4:6],
        grad_up,
        grad_up_bias,
        grad_down,
    )


def solution(mesh):
    placed = (
        P(("dp", "tensor"), None),
        P("dp"),
        P(None, None, "tensor"),
        P(None, "tensor"),
        P("tensor", None),
        P(),
        P(),
        P(),
        P(None, "tensor"),
        P("tensor"),
        P("tensor", None),
        P(("dp", "tensor"), None),
    )
    return jax.shard_map(
        shards,
        mesh=mesh,
        in_specs=placed,
        out_specs=(
            P(("dp", "tensor"), None),
            P(("dp", "tensor"), None),
            P(None, None, "tensor"),
            P(None, "tensor"),
            P("tensor", None),
            P(),
            P(),
            P(),
            P(None, "tensor"),
            P("tensor"),
            P("tensor", None),
        ),
        check_vma=False,
    )
```

```python
import functools
import math

import jax
import jax.numpy as jnp
from jax import lax
from jax.experimental import pallas as pl
from jax.experimental.pallas import tpu as pltpu
from jax.sharding import PartitionSpec as P

D = 1024
H = 16
DOCS_DEV = 4


EPSILON = 1e-06
ROOT_HALF = 0.7071067811865476
GAUSS_NORM = 0.3989422804014327
NT = (((1,), (1,)), ((), ()))
VMEM_ASK = 48 << 20


def norm_forward(summed, gain, shift):
    centred = summed - jnp.mean(summed, axis=-1, keepdims=True)
    inverse = lax.rsqrt(jnp.mean(centred * centred, axis=-1, keepdims=True) + EPSILON)
    unit = centred * inverse
    return (unit * gain + shift, unit, inverse)


def norm_backward(upstream, unit, inverse, gain):
    spread = upstream * gain
    inner = (
        spread
        - jnp.mean(spread, axis=-1, keepdims=True)
        - unit * jnp.mean(spread * unit, axis=-1, keepdims=True)
    )
    return (inner * inverse, jnp.sum(upstream * unit, axis=0), jnp.sum(upstream, axis=0))


def attn_forward_kernel(block, scale, own_ref, rest_ref, seen_ref, bar_ref, *refs):
    mixed_ref, lse_ref = refs[-2:]
    lane = lax.broadcasted_iota(jnp.int32, (1, 128), 1)
    rows = own_ref.shape[1] + rest_ref.shape[1]
    keys = jnp.concatenate([own_ref[1], rest_ref[1]], axis=0)
    values_t = jnp.concatenate([own_ref[2], rest_ref[2]], axis=0).T
    queries = jnp.concatenate([own_ref[0], rest_ref[0]], axis=0) * jnp.bfloat16(scale)
    half = [(lane // 64) == h for h in range(2)]
    keys_of = [jnp.where(half[h], keys, bar_ref[...]) for h in range(2)]
    for first in range(0, rows, block):
        span = slice(first, first + block)
        out_t = []
        for h in range(2):
            query = jnp.where(half[h], queries[span], seen_ref[span])
            scores = lax.dot_general(keys_of[h], query, NT, preferred_element_type=jnp.float32)
            top = jnp.max(scores, axis=0, keepdims=True)
            expd = jnp.exp(scores - top)
            total = jnp.sum(expd, axis=0, keepdims=True)
            mixed = jnp.dot(
                values_t[64 * h : 64 * h + 64],
                expd.astype(jnp.bfloat16),
                preferred_element_type=jnp.float32,
            )
            out_t.append(mixed / total)
            lse_ref[0, h : h + 1, span] = top + jnp.log(total)
        mixed_ref[span] = jnp.concatenate(out_t, axis=0).T.astype(jnp.bfloat16)


def attn_backward_kernel(
    block,
    scale,
    own_ref,
    rest_ref,
    up_own_ref,
    up_rest_ref,
    mixed_ref,
    lse_ref,
    seen_ref,
    bar_ref,
    *refs,
):
    grad_own_ref, grad_rest_ref, key_acc, value_acc = refs[-4:]
    lane = lax.broadcasted_iota(jnp.int32, (1, 128), 1)
    rows_own = own_ref.shape[1]
    rows = rows_own + rest_ref.shape[1]
    keys = jnp.concatenate([own_ref[1], rest_ref[1]], axis=0)
    values = jnp.concatenate([own_ref[2], rest_ref[2]], axis=0)
    keys_t = keys.T
    half = [(lane // 64) == h for h in range(2)]
    keys_of = [jnp.where(half[h], keys, bar_ref[...]) for h in range(2)]
    nothing = jnp.zeros((block, 128), jnp.bfloat16)
    for first in range(0, rows, block):
        span = slice(first, first + block)
        if first < rows_own:
            here, source, up_ref, out_ref = span, own_ref, up_own_ref, grad_own_ref
        else:
            here = slice(first - rows_own, first - rows_own + block)
            source, up_ref, out_ref = rest_ref, up_rest_ref, grad_rest_ref
        query_rows = source[0, here]
        up_rows = up_ref[here]
        product = (up_rows.astype(jnp.float32) * mixed_ref[span].astype(jnp.float32)).T
        query_grad_t = []
        for h in range(2):
            query = jnp.where(half[h], query_rows * jnp.bfloat16(scale), seen_ref[span])
            up = jnp.where(half[h], up_rows, nothing)
            scores = lax.dot_general(keys_of[h], query, NT, preferred_element_type=jnp.float32)
            probs = jnp.exp(scores - lse_ref[0, h : h + 1, span])
            spread = lax.dot_general(values, up, NT, preferred_element_type=jnp.float32)
            inner = jnp.sum(product[64 * h : 64 * h + 64], axis=0, keepdims=True)
            score_grad = (probs * (spread - inner)).astype(jnp.bfloat16)
            value_part = jnp.dot(probs.astype(jnp.bfloat16), up, preferred_element_type=jnp.float32)
            key_part = jnp.dot(
                score_grad, jnp.where(half[h], query_rows, nothing), preferred_element_type=jnp.float32
            )
            if first == 0 and h == 0:
                value_acc[...] = value_part
                key_acc[...] = key_part
            else:
                value_acc[...] += value_part
                key_acc[...] += key_part
            query_grad_t.append(
                jnp.dot(keys_t[64 * h : 64 * h + 64], score_grad, preferred_element_type=jnp.float32)
            )
        out_ref[0, here] = (jnp.concatenate(query_grad_t, axis=0).T * scale).astype(jnp.bfloat16)
    key_low = (key_acc[...] * scale).astype(jnp.bfloat16)
    value_low = value_acc[...].astype(jnp.bfloat16)
    grad_own_ref[1] = key_low[:rows_own]
    grad_rest_ref[1] = key_low[rows_own:]
    grad_own_ref[2] = value_low[:rows_own]
    grad_rest_ref[2] = value_low[rows_own:]


def attn_forward(own, rest, seen, bar, scale, block, start, count, previous=()):
    rows_own, rows_rest, width = own.shape[1], rest.shape[1], own.shape[2]
    rows = rows_own + rows_rest
    return pl.pallas_call(
        functools.partial(attn_forward_kernel, block, scale),
        grid=(count,),
        in_specs=[
            pl.BlockSpec((3, rows_own, 128), lambda p: (0, 0, p + start)),
            pl.BlockSpec((3, rows_rest, 128), lambda p: (0, 0, p + start)),
            pl.BlockSpec((rows, 128), lambda p: (0, 0)),
            pl.BlockSpec((rows, 128), lambda p: (0, 0)),
        ]
        + [pl.BlockSpec(memory_space=pl.ANY)] * len(previous),
        out_specs=[
            pl.BlockSpec((rows, 128), lambda p: (0, p + start)),
            pl.BlockSpec((1, 8, rows), lambda p: (p + start, 0, 0)),
        ],
        out_shape=[
            jax.ShapeDtypeStruct((rows, width), jnp.bfloat16),
            jax.ShapeDtypeStruct((width // 128, 8, rows), jnp.float32),
        ],
        input_output_aliases={4: 0, 5: 1} if previous else {},
        compiler_params=pltpu.CompilerParams(vmem_limit_bytes=VMEM_ASK),
        cost_estimate=pl.CostEstimate(
            flops=count * rows * rows, transcendentals=0, bytes_accessed=count * rows
        ),
        name="attn_forward",
    )(own, rest, seen, bar, *previous)


def attn_backward(
    own, rest, up_own, up_rest, mixed, lse, seen, bar, scale, block, start, count, previous=()
):
    rows_own, rows_rest, width = own.shape[1], rest.shape[1], own.shape[2]
    rows = rows_own + rows_rest
    return pl.pallas_call(
        functools.partial(attn_backward_kernel, block, scale),
        grid=(count,),
        in_specs=[
            pl.BlockSpec((3, rows_own, 128), lambda p: (0, 0, p + start)),
            pl.BlockSpec((3, rows_rest, 128), lambda p: (0, 0, p + start)),
            pl.BlockSpec((rows_own, 128), lambda p: (0, p + start)),
            pl.BlockSpec((rows_rest, 128), lambda p: (0, p + start)),
            pl.BlockSpec((rows, 128), lambda p: (0, p + start)),
            pl.BlockSpec((1, 8, rows), lambda p: (p + start, 0, 0)),
            pl.BlockSpec((rows, 128), lambda p: (0, 0)),
            pl.BlockSpec((rows, 128), lambda p: (0, 0)),
        ]
        + [pl.BlockSpec(memory_space=pl.ANY)] * len(previous),
        out_specs=[
            pl.BlockSpec((3, rows_own, 128), lambda p: (0, 0, p + start)),
            pl.BlockSpec((3, rows_rest, 128), lambda p: (0, 0, p + start)),
        ],
        out_shape=[
            jax.ShapeDtypeStruct((3, rows_own, width), jnp.bfloat16),
            jax.ShapeDtypeStruct((3, rows_rest, width), jnp.bfloat16),
        ],
        input_output_aliases={8: 0, 9: 1} if previous else {},
        scratch_shapes=[pltpu.VMEM((rows, 128), jnp.float32)] * 2,
        compiler_params=pltpu.CompilerParams(vmem_limit_bytes=VMEM_ASK),
        cost_estimate=pl.CostEstimate(
            flops=count * 24 * 256 * rows * rows,
            transcendentals=count * 2 * rows * rows,
            bytes_accessed=count * 18 * 128 * rows,
        ),
        name="attn_backward",
    )(own, rest, up_own, up_rest, mixed, lse, seen, bar, *previous)


def doc_features(docs):
    slot = lax.broadcasted_iota(jnp.int32, (1, 128), 1) % 64
    same = docs[:, None] == slot
    seen = same.astype(jnp.bfloat16)
    bar = jnp.where(same | (slot > 4), 0.0, -(2.0**30)).astype(jnp.bfloat16)
    return seen, bar


def xor_step(array, mask):
    size = lax.axis_size("dp")
    return lax.ppermute(array, "dp", [(i, i ^ mask) for i in range(size)])


def from_rank(array, ahead):
    size = lax.axis_size("tensor")
    return lax.ppermute(array, "tensor", [((i + ahead) % size, i) for i in range(size)])


def exchange(parts):
    size = lax.axis_size("tensor")
    got = [None] * size
    for ahead in range(1, size):
        got[size - ahead] = lax.ppermute(
            parts[ahead], "tensor", [(i, (i + ahead) % size) for i in range(size)]
        )
    return got


def meet(*trees):
    return lax.optimization_barrier(trees)


def spread_kernel(count, order_ref, near_ref, far_ref, out_ref):
    step = pl.program_id(0)
    rows = near_ref.shape[0] // count

    def store(ref):
        for index in range(count):
            offset = pl.multiple_of(order_ref[4 + index] * rows, rows)
            out_ref[pl.ds(offset, rows)] = ref[index * rows : (index + 1) * rows].astype(
                out_ref.dtype
            )

    @pl.when(step < 2)
    def _():
        store(near_ref)

    @pl.when(step > 1)
    def _():
        store(far_ref)


def spread(near, far, place, count, kind):
    rows, columns = near.shape[0] // 2, near.shape[1]
    quarter, inner = lax.div(place, jnp.int32(count)), lax.rem(place, jnp.int32(count))
    order = jnp.concatenate(
        [
            jnp.bitwise_xor(quarter, jnp.arange(4, dtype=jnp.int32)),
            jnp.bitwise_xor(inner, jnp.arange(count, dtype=jnp.int32)),
        ]
    )
    return pl.pallas_call(
        functools.partial(spread_kernel, count),
        grid_spec=pltpu.PrefetchScalarGridSpec(
            num_scalar_prefetch=1,
            grid=(4,),
            in_specs=[
                pl.BlockSpec((rows, columns), lambda step, order: (jnp.minimum(step, 1), 0)),
                pl.BlockSpec((rows, columns), lambda step, order: (jnp.maximum(step - 2, 0), 0)),
            ],
            out_specs=pl.BlockSpec((rows, columns), lambda step, order: (order[step], 0)),
        ),
        out_shape=jax.ShapeDtypeStruct((4 * rows, columns), kind),
        compiler_params=pltpu.CompilerParams(vmem_limit_bytes=VMEM_ASK // 2),
        cost_estimate=pl.CostEstimate(
            flops=0, transcendentals=0, bytes_accessed=24 * rows * columns
        ),
        name="spread_rows",
    )(order, near, far)


def bit_of(dp_pos, mask):
    return jnp.where(lax.bitwise_and(dp_pos, mask) != 0, 1, 0).astype(jnp.int32)


def half_of(array, index):
    rows = array.shape[0] // 2
    return lax.dynamic_slice_in_dim(array, index * rows, rows, 0)


def opening(parts, dp_pos, mask):
    bit = bit_of(dp_pos, mask)
    return [half_of(part, 1 - bit) for part in parts], [half_of(part, bit) for part in parts]


def send(arrays, mask):
    return [xor_step(array, mask) for array in arrays]


def add(keep, got):
    return [
        (a.astype(jnp.float32) + b.astype(jnp.float32)).astype(a.dtype)
        for a, b in zip(keep, got, strict=True)
    ]


def fold(keep, got, dp_pos, mask):
    bit = bit_of(dp_pos, mask)
    away = add([half_of(a, 1 - bit) for a in keep], [half_of(b, 1 - bit) for b in got])
    kept = add([half_of(a, bit) for a in keep], [half_of(b, bit) for b in got])
    return away, kept


def fold_ranks(keep, got):
    total = add(keep, got)
    return [total[0]], exchange(total)[1:]


def add_ranks(keep, got):
    total = keep[0].astype(jnp.float32)
    for piece in got:
        total = total + piece.astype(jnp.float32)
    return total.astype(keep[0].dtype)


def scatter_on(array, dp_pos, masks):
    for mask in masks:
        away, keep = opening([array], dp_pos, mask)
        array = add(keep, send(away, mask))[0]
    return array


def gather_rows(mine, dp_pos, masks):
    for mask in reversed(masks[1:]):
        mine = jnp.concatenate([mine, xor_step(mine, mask)], axis=0)
    place = jnp.int32(0)
    for mask in masks:
        place = 2 * place + bit_of(dp_pos, mask)
    return spread(mine, xor_step(mine, masks[0]), place, 2 ** (len(masks) - 2), jnp.float32)


def butterfly(array, axis):
    size = lax.axis_size(axis)
    mask = 1
    while mask < size:
        array = array + lax.ppermute(array, axis, [(i, i ^ mask) for i in range(size)])
        mask *= 2
    return array


def shards(
    tokens,
    doc_ids,
    w_qkv,
    qv_bias,
    out_weight,
    out_biases,
    ln_gains,
    ln_shifts,
    up_weight,
    up_bias,
    down_weight,
    cotangent,
):
    low = jnp.bfloat16
    rows_own = tokens.shape[0]
    ranks = lax.axis_size("tensor")
    tensor_pos = lax.axis_index("tensor")
    dp_pos = lax.axis_index("dp")
    head_size = D // H
    width = w_qkv.shape[2]
    scale = 1.0 / math.sqrt(head_size)

    count_dp = lax.axis_size("dp")
    masks = [2**k for k in range(count_dp.bit_length() - 1)]
    masks_up = [masks[0], masks[2], masks[1]] + masks[3:]
    others = range(1, ranks)

    rest = [from_rank(tokens, ahead) for ahead in others]
    rest = rest[0] if ranks == 2 else jnp.concatenate(rest, axis=0)
    up_biases = [up_bias] + [from_rank(up_bias, ahead) for ahead in others]
    out_own, up_own, down_own, rest = meet(out_weight, up_weight, down_weight, rest)

    place = 4 * bit_of(dp_pos, 1) + 2 * bit_of(dp_pos, 4) + bit_of(dp_pos, 2)

    def slice_from(weight, pieces, index):
        rows = weight.shape[0] // pieces
        mine = lax.dynamic_slice_in_dim(weight, index * rows, rows, 0)
        return [from_rank(mine, ahead) for ahead in others]

    def joined(groups):
        return [jnp.concatenate(items, axis=0) for items in zip(*groups, strict=True)]

    def corner(by_first, by_second):
        rows = by_first[0].shape[0] // 2
        return (
            [xor_step(item[:rows], 2) for item in by_second],
            [xor_step(item[rows:], 4) for item in by_first],
        )

    out_place = 2 * bit_of(dp_pos, 1) + bit_of(dp_pos, 2)
    out_first, up_first = slice_from(out_own, 4, out_place), slice_from(up_own, 8, place)
    docs = [
        lax.dynamic_slice_in_dim(
            doc_ids, lax.rem(tensor_pos + ahead, ranks) * rows_own, rows_own, 0
        )
        for ahead in range(ranks)
    ]
    seen, bar = doc_features(jnp.concatenate(docs, axis=0))
    bias = jnp.stack([qv_bias[0], jnp.zeros_like(qv_bias[0]), qv_bias[1]])[:, None, :]

    def project(rows):
        wide = jnp.einsum("sd,idc->isc", rows, w_qkv, preferred_element_type=jnp.float32)
        return (wide + bias).astype(low)

    qkv_own, qkv_rest = project(tokens), project(rest)
    qkv_rest, down_own, out_first = meet(qkv_rest, down_own, out_first)
    down_first = slice_from(down_own, 8, place)
    out_second = send(out_first, 2)
    pairs = width // 128
    early = max(1, pairs // 2)
    block = min(512, rows_own)
    mixed_lse = attn_forward(qkv_own, qkv_rest, seen, bar, scale, block, 0, early)
    mixed_lse, out_second, up_first = meet(mixed_lse, out_second, up_first)
    up_second, up_third = send(up_first, 2), send(up_first, 4)
    if pairs > early:
        mixed_lse = attn_forward(
            qkv_own, qkv_rest, seen, bar, scale, block, early, pairs - early, tuple(mixed_lse)
        )
    out_half = joined([out_first, out_second])
    out_far = send(out_half, 1)
    mixed_lse, down_first = meet(mixed_lse, down_first)
    down_second, down_third = send(down_first, 2), send(down_first, 4)
    mixed, lse = mixed_lse
    mixed_parts = [mixed[k * rows_own : (k + 1) * rows_own] for k in range(ranks)]
    mixed_got = exchange(mixed_parts)
    mixed_got[0] = mixed_parts[0]
    mixed_got, out_far, up_second, up_third, up_biases = meet(
        mixed_got, out_far, up_second, up_third, up_biases
    )
    up_corner = corner(up_second, up_third)
    outs = [out_own] + [
        spread(near, far, out_place, 1, low) for near, far in zip(out_half, out_far, strict=True)
    ]
    attention = sum(
        jnp.dot(mixed_got[k], outs[k], preferred_element_type=jnp.float32) for k in range(ranks)
    )
    inputs_own = tokens.astype(jnp.float32)
    normed, unit_first, inverse_first = norm_forward(
        inputs_own + attention + out_biases[0], ln_gains[0], ln_shifts[0]
    )
    normed_low = normed.astype(low)

    def activate(up, up_bias):
        hidden = jnp.dot(normed_low, up, preferred_element_type=jnp.float32) + up_bias
        below = 0.5 * (1.0 + lax.erf(hidden * ROOT_HALF))
        density = jnp.exp(-0.5 * hidden * hidden) * GAUSS_NORM
        return meet((hidden * below).astype(low), (below + hidden * density).astype(low))

    pairs_active = [activate(up_own, up_bias)]
    pairs_active, up_corner, down_second, down_third = meet(
        pairs_active, up_corner, down_second, down_third
    )
    up_half = joined([up_first, up_second, up_third, *up_corner])
    up_far = send(up_half, 1)
    down_corner = corner(down_second, down_third)
    branch = jnp.dot(pairs_active[0][0], down_own, preferred_element_type=jnp.float32)
    branch, up_far, down_corner = meet(branch, up_far, down_corner)
    down_half = joined([down_first, down_second, down_third, *down_corner])
    down_far = send(down_half, 1)
    ups = [up_own] + [
        spread(near, far, place, 2, low) for near, far in zip(up_half, up_far, strict=True)
    ]
    pairs_active += [activate(ups[k], up_biases[k]) for k in others]
    pairs_active, down_far = meet(pairs_active, down_far)
    downs = [down_own] + [
        spread(near, far, place, 2, low) for near, far in zip(down_half, down_far, strict=True)
    ]
    active, slope = zip(*pairs_active, strict=True)
    for k in others:
        branch = branch + jnp.dot(active[k], downs[k], preferred_element_type=jnp.float32)
    result, unit_second, inverse_second = norm_forward(
        normed + branch + out_biases[1], ln_gains[1], ln_shifts[1]
    )

    out_grad = cotangent.astype(jnp.float32) * (docs[0] < DOCS_DEV).astype(jnp.float32)[:, None]
    second_grad, gain_grad_second, shift_grad_second = norm_backward(
        out_grad, unit_second, inverse_second, ln_gains[1]
    )
    bias_grad_second = jnp.sum(second_grad, axis=0)
    branch_grad = second_grad.astype(low)
    down_parts = [
        jnp.einsum("sf,sd->fd", active[k], branch_grad, preferred_element_type=jnp.float32).astype(
            low
        )
        for k in range(ranks)
    ]
    down_parts, branch_grad = meet(down_parts, branch_grad)
    down_away, down_keep = opening(down_parts, dp_pos, masks[0])
    down_away, branch_grad = meet(down_away, branch_grad)
    down_got = send(down_away, masks[0])
    hidden_grads = []
    for k in range(ranks):
        active_grad = jnp.einsum(
            "sd,fd->sf", branch_grad, downs[k], preferred_element_type=jnp.float32
        )
        hidden_grads.append((active_grad * slope[k].astype(jnp.float32)).astype(low))
    hidden_grads, down_got = meet(hidden_grads, down_got)
    down_away, down_keep = fold(down_keep, down_got, dp_pos, masks[1])
    down_away, hidden_grads = meet(down_away, hidden_grads)
    down_got = send(down_away, masks[1])
    up_parts = [
        jnp.einsum(
            "sd,sf->df", normed_low, hidden_grads[k], preferred_element_type=jnp.float32
        ).astype(low)
        for k in range(ranks)
    ]
    up_away, up_keep = opening(up_parts, dp_pos, masks_up[0])
    up_away, hidden_grads = meet(up_away, hidden_grads)
    up_got = send(up_away, masks_up[0])
    normed_grad = second_grad
    for k in range(ranks):
        normed_grad = normed_grad + jnp.einsum(
            "sf,df->sd", hidden_grads[k], ups[k], preferred_element_type=jnp.float32
        )
    first_grad, gain_grad_first, shift_grad_first = norm_backward(
        normed_grad, unit_first, inverse_first, ln_gains[0]
    )
    bias_grad_first = jnp.sum(first_grad, axis=0)
    attn_grad = first_grad.astype(low)
    mixed_grads = [
        jnp.einsum("sd,cd->sc", attn_grad, outs[k], preferred_element_type=jnp.float32).astype(low)
        for k in range(ranks)
    ]
    mixed_grads, up_got = meet(mixed_grads, up_got)
    grads_got = exchange(mixed_grads)
    up_away, up_keep = fold(up_keep, up_got, dp_pos, masks_up[1])
    up_got = send(up_away, masks_up[1])
    out_parts = [
        jnp.einsum("sc,sd->cd", mixed_got[k], attn_grad, preferred_element_type=jnp.float32).astype(
            low
        )
        for k in range(ranks)
    ]
    out_away, out_keep = opening(out_parts, dp_pos, masks[0])
    out_away, grads_got = meet(out_away, grads_got[1:])
    out_got = send(out_away, masks[0])
    grads_rest = grads_got[0] if ranks == 2 else jnp.concatenate(grads_got, axis=0)
    block = min(256, rows_own)
    qkv_grads = attn_backward(
        qkv_own, qkv_rest, mixed_grads[0], grads_rest, mixed, lse, seen, bar, scale, block, 0, early
    )
    qkv_grads, down_got, out_got = meet(qkv_grads, down_got, out_got)
    down_keep, down_got = fold_ranks(down_keep, down_got)
    out_away, out_keep = fold(out_keep, out_got, dp_pos, masks[1])
    out_got = send(out_away, masks[1])
    if pairs > early:
        qkv_grads = attn_backward(
            qkv_own,
            qkv_rest,
            mixed_grads[0],
            grads_rest,
            mixed,
            lse,
            seen,
            bar,
            scale,
            block,
            early,
            pairs - early,
            tuple(qkv_grads),
        )
    qkv_grads, down_got, up_got, out_got = meet(qkv_grads, down_got, up_got, out_got)
    down_sum = add_ranks(down_keep, down_got)
    down_away, down_keep = opening([down_sum], dp_pos, masks[2])
    down_got = send(down_away, masks[2])
    up_keep, up_got = fold_ranks(up_keep, up_got)
    out_keep, out_got = fold_ranks(out_keep, out_got)
    qkv_grad_own, qkv_grad_rest = qkv_grads

    def input_part(item):
        return jnp.einsum("isc,idc->sd", item, w_qkv, preferred_element_type=jnp.float32)

    grad_qkv = jnp.einsum("sd,isc->idc", rest, qkv_grad_rest, preferred_element_type=jnp.float32)
    grad_qkv = grad_qkv + jnp.einsum(
        "sd,isc->idc", tokens, qkv_grad_own, preferred_element_type=jnp.float32
    )
    qkv_away, qkv_keep = opening([grad_qkv.astype(low).reshape(3 * D, width)], dp_pos, masks[0])
    qkv_got = send(qkv_away, masks[0])
    far = input_part(qkv_grad_rest).astype(low)
    far, qkv_got, down_got = meet(far, qkv_got, down_got)
    qkv_away, qkv_keep = fold(qkv_keep, qkv_got, dp_pos, masks[1])
    qkv_got = send(qkv_away, masks[1])
    down_sum = scatter_on(add(down_keep, down_got)[0], dp_pos, masks[3:])
    near = input_part(qkv_grad_own)
    near, up_got, far = meet(near, up_got, far)
    inputs_got = exchange(
        [None] + [far[k * rows_own : (k + 1) * rows_own] for k in range(ranks - 1)]
    )
    up_sum = scatter_on(add_ranks(up_keep, up_got), dp_pos, masks_up[2:])
    qkv_sum = scatter_on(add(qkv_keep, qkv_got)[0], dp_pos, masks[2:])
    grad_down = gather_rows(down_sum, dp_pos, masks)
    grad_up = gather_rows(up_sum, dp_pos, masks_up)
    grad_qkv = gather_rows(qkv_sum, dp_pos, masks)
    out_sum = add_ranks(out_keep, out_got)
    if (out_sum.shape[0] * 4 // count_dp) % 16 == 0:
        grad_out = gather_rows(scatter_on(out_sum, dp_pos, masks[2:]), dp_pos, masks)
    else:
        for mask in masks[2:]:
            out_sum = add([out_sum], send([out_sum], mask))[0]
        half = jnp.concatenate([out_sum, xor_step(out_sum, masks[1])], axis=0)
        grad_out = spread(half, xor_step(half, masks[0]), out_place, 1, jnp.float32)

    up_sums = [jnp.sum(item.astype(jnp.float32), axis=0) for item in hidden_grads]
    sums_got = exchange(up_sums)
    hidden_sum = up_sums[0]
    for piece in sums_got[1:]:
        hidden_sum = hidden_sum + piece
    shared = butterfly(
        jnp.stack(
            [
                bias_grad_first,
                bias_grad_second,
                gain_grad_first,
                gain_grad_second,
                shift_grad_first,
                shift_grad_second,
            ]
        ),
        "tensor",
    )
    shared = butterfly(jnp.concatenate([shared.reshape(-1), hidden_sum]), "dp")
    shared, grad_up_bias = shared[: 6 * D].reshape(6, D), shared[6 * D :]
    qkv_sums = jnp.sum(qkv_grad_own.astype(jnp.float32), axis=1) + jnp.sum(
        qkv_grad_rest.astype(jnp.float32), axis=1
    )
    grad_qv = butterfly(jnp.stack([qkv_sums[0], qkv_sums[2]]), "dp")
    grad_input = first_grad + near
    for piece in inputs_got[1:]:
        grad_input = grad_input + piece.astype(jnp.float32)
    return (
        result.astype(low),
        grad_input.astype(low),
        grad_qkv.reshape(3, D, width),
        grad_qv,
        grad_out,
        shared[0:2],
        shared[2:4],
        shared[4:6],
        grad_up,
        grad_up_bias,
        grad_down,
    )


def solution(mesh):
    placed = (
        P(("dp", "tensor"), None),
        P("dp"),
        P(None, None, "tensor"),
        P(None, "tensor"),
        P("tensor", None),
        P(),
        P(),
        P(),
        P(None, "tensor"),
        P("tensor"),
        P("tensor", None),
        P(("dp", "tensor"), None),
    )
    return jax.shard_map(
        shards,
        mesh=mesh,
        in_specs=placed,
        out_specs=(
            P(("dp", "tensor"), None),
            P(("dp", "tensor"), None),
            P(None, None, "tensor"),
            P(None, "tensor"),
            P("tensor", None),
            P(),
            P(),
            P(),
            P(None, "tensor"),
            P("tensor"),
            P("tensor", None),
        ),
        check_vma=False,
    )
```
